32 devices in a mesh: req: 8 (over y, x, core), cand: 4 (over z).
Axes of the slice: x: 2, y: 2, z: 4, core: 2. Of those that a mesh axis runs over, the one named last changes fastest.
Arguments:
- history: bfloat16 [64, 256, 1024], P('req', 'cand'), may hold values from -6 to 6
- history_length: int32 [64], P('req'), may hold values from 32 to 256
- candidate_count: int32 [64], P('req'), may hold values from 512 to 4096
- block_shard: int32 [64, 32], P('req'), may hold values from 0 to 3, as said below
- block_index: int32 [64, 32], P('req'), may hold values from 0 to 3
- item_table: bfloat16 [16, 128, 1024], P('cand'), may hold values from -6 to 6
- item_ages: int32 [64, 4096], P('req', 'cand'), may hold values from 0 to 336
- history_weight: bfloat16 [1024, 2048], P('req'), may hold values from -0.1875 to 0.1875
- candidate_weight: bfloat16 [1024, 2048], P('req'), may hold values from -0.1875 to 0.1875
- output_weight: bfloat16 [1024, 1024], P('req'), may hold values from -0.1875 to 0.1875
- hidden_weight: bfloat16 [1024, 256], P('req'), may hold values from -0.1875 to 0.1875
- norm_gain: float32 [1024], replicated, may hold values from 0.1 to 1.9
- score_weight: bfloat16 [2, 256], replicated, may hold values from -0.375 to 0.375
Outputs:
- scores: float32 [64, 4096], P('req', 'cand')
The draws below stay inside these ranges and needn't reach their ends.
Inputs may be any that keep to these rules, and one draw needn't show every extreme that they name: `block_shard`: for each group of 8 consecutive requests (aligned) and each c, the slots j with j // 8 == c of those requests name every shard exactly 16 times.
All inputs are finite; a program needn't handle non-finite values.
Results may differ from the reference program's by a relative error of at most 0.0053.
Values may be sent and summed in bfloat16 or wider, within the bound.
A program may use at most 128 MiB of HBM per device.

```python
import math
import jax
import jax.numpy as jnp
from jax import lax

D = 1024
HEADS = 8
MLPH = 256
HIST = 256
R_DEV = 8
MAXB = 32
MINB = 4
BLOCK = 128
IB_DEV = 4
REQS = 64
SHARDS = 4
MAXC = 4096
ITEM_BLOCKS = 16
CAP = 16


def draw_history_length(key, part):
    first, second = jax.random.split(key)
    values = jax.random.randint(first, (REQS,), HIST // 8, HIST + 1)
    spot = jax.random.randint(second, (), 0, REQS)
    return jnp.where(jnp.arange(REQS) == spot, HIST, values).astype(jnp.int32)


def draw_candidate_count(key, part):
    first, second = jax.random.split(key)
    values = jax.random.randint(first, (REQS,), MINB * BLOCK, MAXC + 1)
    spot = jax.random.randint(second, (), 0, REQS)
    return jnp.where(jnp.arange(REQS) == spot, MAXC, values).astype(jnp.int32)


def draw_block_shard(key, part):
    groups = REQS // R_DEV
    per_scorer = MAXB // SHARDS
    slot_count = R_DEV * per_scorer
    ranks = jax.random.randint(key, (groups * SHARDS, slot_count), 0, 1 << 20)
    ranks = ranks * slot_count + jnp.arange(slot_count, dtype=jnp.int32)[None, :]
    order = jnp.argsort(ranks, axis=1, stable=True)
    base = jnp.arange(slot_count, dtype=jnp.int32) // CAP
    shards = base[order]
    shards = shards.reshape(groups, SHARDS, R_DEV, per_scorer).transpose(0, 2, 1, 3)
    return shards.reshape(REQS, MAXB).astype(jnp.int32)


def set_ends(entries, rng, low, top_value):
    longest = entries.shape.index(max(entries.shape))
    spots = []
    for shift in (0, 1):
        where = [jax.random.randint(jax.random.fold_in(rng, axis), (), 0, length) for axis, length in enumerate(entries.shape)]
        where[longest] = (where[longest] + shift) % entries.shape[longest]
        spots.append(tuple(where))
    return entries.at[spots[0]].set(low).at[spots[1]].set(top_value)


def shard_levels(key, shape, pieces, least, high):
    loudness = 1.0
    for dim, shards_of in pieces:
        heights = jax.random.uniform(jax.random.fold_in(jax.random.fold_in(key, 6), dim), (shards_of,), jnp.float32, least / len(pieces), high / len(pieces))
        loudness = loudness * jnp.repeat(jnp.exp(heights), shape[dim] // shards_of).reshape((-1,) + (1,) * (len(shape) - 1 - dim))
    return loudness


def noise(key, dims, width, reach, pieces=(), held_as=jnp.bfloat16):
    array = width * jax.random.normal(key, dims, jnp.float32)
    if pieces:
        array = array * shard_levels(key, dims, pieces, -0.22, 0.18)
    return jnp.clip(array, -reach, reach).astype(held_as)


def setup_inputs(seed: int = 0) -> dict:
    key_of = jax.random.split(jax.random.key(seed), 14)
    history = noise(key_of[0], (REQS, HIST, D), 1.0, 6.0, ((0, 8), (1, 4)))
    history_length = draw_history_length(jax.random.fold_in(key_of[13], 71), 0)
    candidate_count = draw_candidate_count(jax.random.fold_in(key_of[13], 71), 0)
    block_shard = draw_block_shard(jax.random.fold_in(key_of[13], 71), 0)
    block_index = set_ends(jax.random.randint(key_of[4], (REQS, MAXB), 0, IB_DEV), jax.random.fold_in(key_of[4], 1), 0, IB_DEV - 1).astype(jnp.int32)
    item_table = noise(key_of[5], (ITEM_BLOCKS, BLOCK, D), 1.0, 6.0, ((0, 4),))
    item_ages = set_ends(jax.random.randint(key_of[6], (REQS, MAXC), 0, 337), jax.random.fold_in(key_of[6], 1), 0, 336).astype(jnp.int32)
    history_weight = noise(key_of[7], (D, 2 * D), D ** -0.5, 0.1875, ((0, 8),))
    candidate_weight = noise(key_of[8], (D, 2 * D), D ** -0.5, 0.1875, ((0, 8),))
    output_weight = noise(key_of[9], (D, D), D ** -0.5, 0.1875, ((0, 8),))
    hidden_weight = noise(key_of[10], (D, MLPH), D ** -0.5, 0.1875, ((0, 8),))
    norm_gain = jnp.clip(1.0 + 0.18 * jax.random.normal(key_of[11], (D,), jnp.float32), 0.1, 1.9)
    score_weight = noise(key_of[12], (2, MLPH), MLPH ** -0.5, 0.375)
    return {"history": history, "history_length": history_length, "candidate_count": candidate_count, "block_shard": block_shard, "block_index": block_index, "item_table": item_table, "item_ages": item_ages, "history_weight": history_weight, "candidate_weight": candidate_weight, "output_weight": output_weight, "hidden_weight": hidden_weight, "norm_gain": norm_gain, "score_weight": score_weight}


EPSILON = 1e-05
AGE_SCALE = 48.0

def rounded(value):
    return lax.optimization_barrier(value.astype(jnp.bfloat16)).astype(jnp.float32)

def reference(history, history_length, candidate_count, block_shard, block_index, item_table, item_ages, history_weight, candidate_weight, output_weight, hidden_weight, norm_gain, score_weight):
    head_size = D // HEADS
    score_scale = 1.0 / math.sqrt(head_size)
    query_weight = candidate_weight[:, :D]
    gate_weight = candidate_weight[:, D:]
    positions = jnp.arange(HIST, dtype=jnp.int32)

    def one_request(operands):
        history_rows, length, row_count, sources, indices, age_rows = operands
        projected = jax.nn.silu(jnp.dot(history_rows, history_weight, preferred_element_type=jnp.float32))
        projected = rounded(projected)
        key_rows = projected[:, :D].reshape(HIST, HEADS, head_size)
        value_rows = projected[:, D:].reshape(HIST, HEADS, head_size)
        blocks = item_table[(sources * IB_DEV + indices).astype(jnp.int32)]

        def one_block(block_ops):
            block_rows, number, block_ages = block_ops

            def score_block(block_rows):
                query = rounded(jax.nn.silu(jnp.dot(block_rows, query_weight, preferred_element_type=jnp.float32)))
                query = query.reshape(BLOCK, HEADS, head_size)
                scores = jnp.einsum('ihd,phd->hip', query, key_rows) * score_scale
                weights = jax.nn.silu(scores) / length.astype(jnp.float32)
                weights = rounded(jnp.where(positions[None, None, :] < length, weights, 0.0))
                attended = jnp.einsum('hip,phd->ihd', weights, value_rows).reshape(BLOCK, D)
                gate = jax.nn.silu(jnp.dot(block_rows, gate_weight, preferred_element_type=jnp.float32))
                center = attended - lax.optimization_barrier(jnp.mean(attended, axis=-1, keepdims=True))
                spread = lax.optimization_barrier(jnp.mean(center * center, axis=-1, keepdims=True))
                normed = (center * lax.rsqrt(spread + EPSILON) * norm_gain * gate).astype(jnp.bfloat16)
                merged = (jnp.dot(normed, output_weight, preferred_element_type=jnp.float32) + block_rows.astype(jnp.float32)).astype(jnp.bfloat16)
                hidden = jax.nn.silu(jnp.dot(merged, hidden_weight, preferred_element_type=jnp.float32)).astype(jnp.bfloat16)
                logits = jnp.einsum('ik,ck->ci', hidden.astype(jnp.float32), score_weight.astype(jnp.float32))
                decays = jnp.exp(-block_ages.astype(jnp.float32) / AGE_SCALE)
                blended = decays * logits[0] + (1.0 - decays) * logits[1]
                kept_rows = number * BLOCK + jnp.arange(BLOCK, dtype=jnp.int32) < row_count
                return jnp.where(kept_rows, blended, 0.0)

            def empty_block(block_rows):
                return jnp.zeros((BLOCK,), jnp.float32)
            return lax.cond(number * BLOCK < row_count, score_block, empty_block, block_rows)
        return lax.map(one_block, (blocks, jnp.arange(MAXB, dtype=jnp.int32), age_rows.reshape(MAXB, BLOCK)))
    result = lax.map(one_request, (history, history_length, candidate_count, block_shard, block_index, item_ages))
    return result.reshape(REQS, MAXC)
```

```python
import math

import jax
import jax.numpy as jnp
from jax import lax
from jax.experimental import pallas as pl
from jax.experimental.pallas import tpu as pltpu
from jax.sharding import PartitionSpec as P

HEADS = 8
BLOCK = 128
EPSILON = 1e-05
AGE_SCALE = 48.0


def silu(value):
    half = 0.5 * value
    return half + half * jnp.tanh(half)


def pair_kernel(
    length_ref,
    history_ref,
    items_ref,
    history_weight_ref,
    candidate_weight_ref,
    output_weight_ref,
    hidden_weight_ref,
    gain_ref,
    score_weight_ref,
    logits_ref,
    query_ref,
    gate_ref,
    pairs_ref,
    attended_ref,
):
    request = pl.program_id(0)
    rows, width = items_ref.shape
    head = width // HEADS
    history_total = history_ref.shape[1]
    half_scale = 0.5 / math.sqrt(head)

    @pl.when(request == 0)
    def _():
        query_ref[...] = silu(
            jnp.dot(
                items_ref[...],
                candidate_weight_ref[:, :width],
                preferred_element_type=jnp.float32,
            )
        ).astype(jnp.bfloat16)
        gate_ref[...] = (
            silu(
                jnp.dot(
                    items_ref[...],
                    candidate_weight_ref[:, width:],
                    preferred_element_type=jnp.float32,
                )
            )
            * gain_ref[...]
        )

    length = length_ref[request]
    inverse = 1.0 / jnp.full((1, 1), length, jnp.int32).astype(jnp.float32)
    pairs_ref[:, :width] = silu(
        jnp.dot(
            history_ref[0], history_weight_ref[:, :width], preferred_element_type=jnp.float32
        )
    ).astype(jnp.bfloat16)
    live = lax.broadcasted_iota(jnp.int32, (history_total, width), 0) < length
    pairs_ref[:, width:] = jnp.where(
        live,
        silu(
            jnp.dot(
                history_ref[0], history_weight_ref[:, width:], preferred_element_type=jnp.float32
            )
        ),
        0.0,
    ).astype(jnp.bfloat16)
    for h in range(HEADS):
        part = slice(h * head, (h + 1) * head)
        scores = half_scale * lax.dot_general(
            query_ref[:, part],
            pairs_ref[:, part],
            (((1,), (1,)), ((), ())),
            preferred_element_type=jnp.float32,
        )
        weights = ((scores + scores * jnp.tanh(scores)) * inverse).astype(jnp.bfloat16)
        attended_ref[:, part] = jnp.dot(
            weights,
            pairs_ref[:, width + h * head : width + (h + 1) * head],
            preferred_element_type=jnp.float32,
        )
    attended = attended_ref[...]
    center = attended - jnp.mean(attended, axis=-1, keepdims=True)
    spread = jnp.mean(center * center, axis=-1, keepdims=True)
    normed = (center * lax.rsqrt(spread + EPSILON) * gate_ref[...]).astype(jnp.bfloat16)
    merged = (
        jnp.dot(normed, output_weight_ref[...], preferred_element_type=jnp.float32)
        + items_ref[...].astype(jnp.float32)
    ).astype(jnp.bfloat16)
    hidden = silu(
        jnp.dot(merged, hidden_weight_ref[...], preferred_element_type=jnp.float32)
    ).astype(jnp.bfloat16)
    logits_ref[0] = lax.dot_general(
        score_weight_ref[...],
        hidden,
        (((1,), (1,)), ((), ())),
        preferred_element_type=jnp.float32,
    )


def pair_logits(
    history, length, items, history_weight, candidate_weight, output_weight, hidden_weight, gain,
    score_weight,
):
    requests, history_total, width = history.shape
    rows = items.shape[0]
    whole = pl.BlockSpec(memory_space=pltpu.VMEM)
    return pl.pallas_call(
        pair_kernel,
        out_shape=jax.ShapeDtypeStruct((requests, score_weight.shape[0], rows), jnp.float32),
        grid=(requests,),
        in_specs=[
            pl.BlockSpec(memory_space=pltpu.SMEM),
            pl.BlockSpec((1, history_total, width), lambda i: (i, 0, 0)),
            whole, whole, whole, whole, whole, whole, whole,
        ],
        out_specs=pl.BlockSpec((1, score_weight.shape[0], rows), lambda i: (i, 0, 0)),
        scratch_shapes=[
            pltpu.VMEM((rows, width), jnp.bfloat16),
            pltpu.VMEM((rows, width), jnp.float32),
            pltpu.VMEM((history_total, 2 * width), jnp.bfloat16),
            pltpu.VMEM((rows, width), jnp.float32),
        ],
        compiler_params=pltpu.CompilerParams(vmem_limit_bytes=56 * 1024 * 1024),
    )(
        length, history, items, history_weight, candidate_weight, output_weight, hidden_weight,
        gain, score_weight,
    )


def blend(logits, candidate_count, block_shard, block_index, item_ages, item_blocks):
    shards = lax.axis_size("cand")
    mine = lax.axis_index("cand")
    requests, max_blocks = block_shard.shape
    per_scorer = max_blocks // shards
    logits = logits.reshape(shards, requests, -1, item_blocks, BLOCK)
    ids = lax.dynamic_slice_in_dim(
        block_shard * item_blocks + block_index, mine * per_scorer, per_scorer, 1
    )
    names = jnp.arange(shards * item_blocks, dtype=jnp.int32).reshape(shards, 1, 1, item_blocks, 1)
    picked = ids[None, :, :, None, None] == names
    first, second = (
        jnp.sum(jnp.where(picked, logits[:, :, None, c], 0.0), axis=(0, 3)) for c in (0, 1)
    )
    decays = jnp.exp(
        -item_ages.astype(jnp.float32).reshape(requests, per_scorer, BLOCK) / AGE_SCALE
    )
    blended = decays * first + (1.0 - decays) * second
    row_number = (mine * per_scorer + jnp.arange(per_scorer, dtype=jnp.int32))[
        None, :, None
    ] * BLOCK + jnp.arange(BLOCK, dtype=jnp.int32)[None, None, :]
    kept_rows = row_number < candidate_count[:, None, None]
    return jnp.where(kept_rows, blended, 0.0).reshape(requests, per_scorer * BLOCK)


def local(
    history,
    history_length,
    candidate_count,
    block_shard,
    block_index,
    item_table,
    item_ages,
    history_weight,
    candidate_weight,
    output_weight,
    hidden_weight,
    norm_gain,
    score_weight,
):
    proj = [
        lax.all_gather(weight, "req", axis=0, tiled=True)
        for weight in (history_weight, candidate_weight, output_weight, hidden_weight)
    ]
    full_history = lax.all_gather(history, "cand", axis=1, tiled=True)
    item_blocks = item_table.shape[0]
    logits = pair_logits(
        full_history,
        history_length,
        item_table.reshape(-1, item_table.shape[2]),
        *proj,
        norm_gain[None, :],
        score_weight,
    )
    logits = lax.all_gather(logits, "cand", axis=0, tiled=True)
    return blend(logits, candidate_count, block_shard, block_index, item_ages, item_blocks)


def solution(mesh):
    return jax.shard_map(
        local,
        mesh=mesh,
        in_specs=(
            P("req", "cand", None),
            P("req"),
            P("req"),
            P("req", None),
            P("req", None),
            P("cand", None, None),
            P("req", "cand"),
            P("req", None),
            P("req", None),
            P("req", None),
            P("req", None),
            P(),
            P(),
        ),
        out_specs=P("req", "cand"),
        check_vma=False,
    )
```

```python
import functools
import math

import jax
import jax.numpy as jnp
from jax import lax
from jax.experimental import pallas as pl
from jax.experimental.pallas import tpu as pltpu
from jax.sharding import PartitionSpec as P

HEADS = 8
BLOCK = 128
EPSILON = 1e-05
AGE_SCALE = 48.0


def silu(value):
    half = 0.5 * value
    return half + half * jnp.tanh(half)


MESH = pl.DeviceIdType.MESH


def pair_kernel(
    groups,
    shards,
    length_ref,
    history_ref,
    items_ref,
    history_shard_ref,
    candidate_shard_ref,
    output_shard_ref,
    hidden_shard_ref,
    gain_ref,
    score_weight_ref,
    logits_ref,
    events_ref,
    history_weight_ref,
    candidate_weight_ref,
    output_weight_ref,
    hidden_weight_ref,
    query_ref,
    gate_ref,
    pairs_ref,
    attended_ref,
    weight_send,
    weight_recv,
    pass_send,
    event_send,
    event_recv,
    logit_send,
    logit_recv,
    own_sem,
):
    group = lax.axis_index("req")
    shard = lax.axis_index("cand")
    partner = group + 1 - 2 * lax.rem(group, 2)
    requests, own_events, width = history_ref.shape
    history_total = events_ref.shape[1]
    head = width // HEADS
    half_scale = 0.5 / math.sqrt(head)
    weights = (
        (candidate_shard_ref, candidate_weight_ref),
        (history_shard_ref, history_weight_ref),
        (output_shard_ref, output_weight_ref),
        (hidden_shard_ref, hidden_weight_ref),
    )
    depth = history_shard_ref.shape[0]
    same_core = [lax.rem(group + 2 * d, groups) for d in range(1, groups // 2)]
    partner_core = [lax.rem(partner + 2 * d, groups) for d in range(1, groups // 2)]
    others = [lax.rem(shard + d, shards) for d in range(1, shards)]

    def rows_of(source):
        return pl.ds(pl.multiple_of(source * depth, depth), depth)

    def events_of(source):
        return pl.ds(pl.multiple_of(source * own_events, own_events), own_events)

    def weight_copy(w, target, source, send):
        part, full = weights[w]
        return pltpu.make_async_remote_copy(
            src_ref=part,
            dst_ref=full.at[rows_of(source)],
            send_sem=send,
            recv_sem=weight_recv.at[w, source],
            device_id={"req": target},
            device_id_type=MESH,
        )

    def pass_copy(w, k, source):
        full = weights[w][1]
        return pltpu.make_async_remote_copy(
            src_ref=full.at[rows_of(source)],
            dst_ref=full.at[rows_of(source)],
            send_sem=pass_send.at[w, k],
            recv_sem=weight_recv.at[w, source],
            device_id={"req": partner},
            device_id_type=MESH,
        )

    def event_copy(i, k, target, source):
        return pltpu.make_async_remote_copy(
            src_ref=history_ref.at[i],
            dst_ref=events_ref.at[i, events_of(source)],
            send_sem=event_send.at[i, k],
            recv_sem=event_recv.at[i, source],
            device_id={"cand": target},
            device_id_type=MESH,
        )

    def logit_copy(i, k, target, source):
        return pltpu.make_async_remote_copy(
            src_ref=logits_ref.at[source, i],
            dst_ref=logits_ref.at[source, i],
            send_sem=logit_send.at[i, k],
            recv_sem=logit_recv.at[i, source],
            device_id={"cand": target},
            device_id_type=MESH,
        )

    def own_weight(w):
        part, full = weights[w]
        return pltpu.make_async_copy(part, full.at[rows_of(group)], own_sem.at[w])

    def own_event(i):
        return pltpu.make_async_copy(
            history_ref.at[i], events_ref.at[i, events_of(shard)], own_sem.at[len(weights) + i]
        )

    barrier = pltpu.get_barrier_semaphore()
    for target in (*same_core, partner):
        pl.semaphore_signal(barrier, inc=1, device_id={"req": target}, device_id_type=MESH)
    for target in others:
        pl.semaphore_signal(barrier, inc=1, device_id={"cand": target}, device_id_type=MESH)
    pl.semaphore_wait(barrier, len(same_core) + 1 + len(others))

    for w in range(len(weights)):
        for k, target in enumerate(same_core):
            weight_copy(w, target, group, weight_send.at[w, k]).start()
        weight_copy(w, partner, group, weight_send.at[w, len(same_core)]).start()
        own_weight(w).start()

    @pl.loop(0, requests)
    def _(i):
        for k, target in enumerate(others):
            event_copy(i, k, target, shard).start()
        own_event(i).start()

    def pass_on(w):
        for k, source in enumerate(same_core):
            weight_copy(w, partner, source, weight_send.at[w, k]).wait_recv()
            pass_copy(w, k, source).start()

    def settle(w):
        own_weight(w).wait()
        for source in (partner, *partner_core):
            weight_copy(w, partner, source, weight_send.at[w, 0]).wait_recv()

    pass_on(0)
    settle(0)
    query_ref[...] = silu(
        jnp.dot(
            items_ref[...], candidate_weight_ref[:, :width], preferred_element_type=jnp.float32
        )
    ).astype(jnp.bfloat16)
    gate_ref[...] = (
        silu(
            jnp.dot(
                items_ref[...], candidate_weight_ref[:, width:], preferred_element_type=jnp.float32
            )
        )
        * gain_ref[...]
    )
    for w in range(1, len(weights)):
        pass_on(w)
    for w in range(1, len(weights)):
        settle(w)

    @pl.loop(0, requests)
    def _(i):
        own_event(i).wait()
        for k, source in enumerate(others):
            event_copy(i, k, source, source).wait_recv()
        length = length_ref[i]
        inverse = 1.0 / jnp.full((1, 1), length, jnp.int32).astype(jnp.float32)
        pairs_ref[:, :width] = silu(
            jnp.dot(
                events_ref[i], history_weight_ref[:, :width], preferred_element_type=jnp.float32
            )
        ).astype(jnp.bfloat16)
        live = lax.broadcasted_iota(jnp.int32, (history_total, width), 0) < length
        pairs_ref[:, width:] = jnp.where(
            live,
            silu(
                jnp.dot(
                    events_ref[i], history_weight_ref[:, width:], preferred_element_type=jnp.float32
                )
            ),
            0.0,
        ).astype(jnp.bfloat16)
        for h in range(HEADS):
            part = slice(h * head, (h + 1) * head)
            scores = half_scale * lax.dot_general(
                query_ref[:, part],
                pairs_ref[:, part],
                (((1,), (1,)), ((), ())),
                preferred_element_type=jnp.float32,
            )
            mixed = ((scores + scores * jnp.tanh(scores)) * inverse).astype(jnp.bfloat16)
            attended_ref[:, part] = jnp.dot(
                mixed,
                pairs_ref[:, width + h * head : width + (h + 1) * head],
                preferred_element_type=jnp.float32,
            )

        @pl.when(i > 0)
        def _():
            for k, target in enumerate(others):
                logit_copy(i - 1, k, target, shard).start()

        attended = attended_ref[...]
        center = attended - jnp.mean(attended, axis=-1, keepdims=True)
        spread = jnp.mean(center * center, axis=-1, keepdims=True)
        normed = (center * lax.rsqrt(spread + EPSILON) * gate_ref[...]).astype(jnp.bfloat16)
        merged = (
            jnp.dot(normed, output_weight_ref[...], preferred_element_type=jnp.float32)
            + items_ref[...].astype(jnp.float32)
        ).astype(jnp.bfloat16)
        hidden = silu(
            jnp.dot(merged, hidden_weight_ref[...], preferred_element_type=jnp.float32)
        ).astype(jnp.bfloat16)
        logits_ref[shard, i] = lax.dot_general(
            score_weight_ref[...],
            hidden,
            (((1,), (1,)), ((), ())),
            preferred_element_type=jnp.float32,
        )

    for w in range(len(weights)):
        for k, target in enumerate((*same_core, partner)):
            weight_copy(w, target, group, weight_send.at[w, k]).wait_send()
        for k, source in enumerate(same_core):
            pass_copy(w, k, source).wait_send()

    @pl.loop(0, requests)
    def _(i):
        for k, target in enumerate(others):
            event_copy(i, k, target, shard).wait_send()

    for k, target in enumerate(others):
        logit_copy(requests - 1, k, target, shard).start()

    @pl.loop(0, requests)
    def _(i):
        for k, target in enumerate(others):
            logit_copy(i, k, target, shard).wait_send()
            logit_copy(i, k, target, target).wait_recv()


def pair_logits(
    history, length, items, history_weight, candidate_weight, output_weight, hidden_weight, gain,
    score_weight,
):
    requests, own_events, width = history.shape
    rows = items.shape[0]
    groups, shards = lax.axis_size("req"), lax.axis_size("cand")
    history_total = own_events * shards
    whole = pl.BlockSpec(memory_space=pltpu.VMEM)
    apart = pl.BlockSpec(memory_space=pl.ANY)
    weights = (history_weight, candidate_weight, output_weight, hidden_weight)
    count = len(weights)
    return pl.pallas_call(
        functools.partial(pair_kernel, groups, shards),
        out_shape=jax.ShapeDtypeStruct((shards, requests, score_weight.shape[0], rows), jnp.float32),
        in_specs=[
            pl.BlockSpec(memory_space=pltpu.SMEM),
            apart, whole, apart, apart, apart, apart, whole, whole,
        ],
        out_specs=whole,
        scratch_shapes=[
            pltpu.VMEM((requests, history_total, width), jnp.bfloat16),
            *(
                pltpu.VMEM((weight.shape[0] * groups, weight.shape[1]), jnp.bfloat16)
                for weight in weights
            ),
            pltpu.VMEM((rows, width), jnp.bfloat16),
            pltpu.VMEM((rows, width), jnp.float32),
            pltpu.VMEM((history_total, 2 * width), jnp.bfloat16),
            pltpu.VMEM((rows, width), jnp.float32),
            pltpu.SemaphoreType.DMA((count, groups // 2)),
            pltpu.SemaphoreType.DMA((count, groups)),
            pltpu.SemaphoreType.DMA((count, groups // 2)),
            pltpu.SemaphoreType.DMA((requests, shards)),
            pltpu.SemaphoreType.DMA((requests, shards)),
            pltpu.SemaphoreType.DMA((requests, shards)),
            pltpu.SemaphoreType.DMA((requests, shards)),
            pltpu.SemaphoreType.DMA((count + requests,)),
        ],
        compiler_params=pltpu.CompilerParams(
            collective_id=0, has_side_effects=True, vmem_limit_bytes=58 * 1024 * 1024
        ),
    )(
        length, history, items, history_weight, candidate_weight, output_weight, hidden_weight,
        gain, score_weight,
    )


def blend(logits, candidate_count, block_shard, block_index, item_ages, item_blocks):
    shards = lax.axis_size("cand")
    mine = lax.axis_index("cand")
    requests, max_blocks = block_shard.shape
    per_scorer = max_blocks // shards
    logits = logits.reshape(shards, requests, -1, item_blocks, BLOCK)
    ids = lax.dynamic_slice_in_dim(
        block_shard * item_blocks + block_index, mine * per_scorer, per_scorer, 1
    )
    names = jnp.arange(shards * item_blocks, dtype=jnp.int32).reshape(shards, 1, 1, item_blocks, 1)
    picked = ids[None, :, :, None, None] == names
    first, second = (
        jnp.sum(jnp.where(picked, logits[:, :, None, c], 0.0), axis=(0, 3)) for c in (0, 1)
    )
    decays = jnp.exp(
        -item_ages.astype(jnp.float32).reshape(requests, per_scorer, BLOCK) / AGE_SCALE
    )
    blended = decays * first + (1.0 - decays) * second
    row_number = (mine * per_scorer + jnp.arange(per_scorer, dtype=jnp.int32))[
        None, :, None
    ] * BLOCK + jnp.arange(BLOCK, dtype=jnp.int32)[None, None, :]
    kept_rows = row_number < candidate_count[:, None, None]
    return jnp.where(kept_rows, blended, 0.0).reshape(requests, per_scorer * BLOCK)


def local(
    history,
    history_length,
    candidate_count,
    block_shard,
    block_index,
    item_table,
    item_ages,
    history_weight,
    candidate_weight,
    output_weight,
    hidden_weight,
    norm_gain,
    score_weight,
):
    item_blocks = item_table.shape[0]
    logits = pair_logits(
        history,
        history_length,
        item_table.reshape(-1, item_table.shape[2]),
        history_weight,
        candidate_weight,
        output_weight,
        hidden_weight,
        norm_gain[None, :],
        score_weight,
    )
    return blend(logits, candidate_count, block_shard, block_index, item_ages, item_blocks)


def solution(mesh):
    return jax.shard_map(
        local,
        mesh=mesh,
        in_specs=(
            P("req", "cand", None),
            P("req"),
            P("req"),
            P("req", None),
            P("req", None),
            P("cand", None, None),
            P("req", "cand"),
            P("req", None),
            P("req", None),
            P("req", None),
            P("req", None),
            P(),
            P(),
        ),
        out_specs=P("req", "cand"),
        check_vma=False,
    )
```

```python
import functools
import math

import jax
import jax.numpy as jnp
from jax import lax
from jax.experimental import pallas as pl
from jax.experimental.pallas import tpu as pltpu
from jax.sharding import PartitionSpec as P

HEADS = 8
BLOCK = 128
EPSILON = 1e-05
AGE_SCALE = 48.0


def silu(value):
    half = 0.5 * value
    return half + half * jnp.tanh(half)


MESH = pl.DeviceIdType.MESH


def pair_kernel(
    groups,
    shards,
    length_ref,
    history_ref,
    items_ref,
    history_shard_ref,
    candidate_shard_ref,
    output_shard_ref,
    hidden_shard_ref,
    gain_ref,
    score_weight_ref,
    logits_ref,
    events_ref,
    history_weight_ref,
    candidate_weight_ref,
    output_weight_ref,
    hidden_weight_ref,
    query_ref,
    gate_ref,
    pairs_ref,
    attended_ref,
    weight_send,
    weight_recv,
    pass_send,
    turn_send,
    event_send,
    event_recv,
    logit_send,
    logit_recv,
    own_sem,
):
    group = lax.axis_index("req")
    shard = lax.axis_index("cand")
    partner = group + 1 - 2 * lax.rem(group, 2)
    requests, own_events, width = history_ref.shape
    history_total = events_ref.shape[1]
    head = width // HEADS
    half_scale = 0.5 / math.sqrt(head)
    weights = (
        (candidate_shard_ref, candidate_weight_ref),
        (history_shard_ref, history_weight_ref),
        (output_shard_ref, output_weight_ref),
        (hidden_shard_ref, hidden_weight_ref),
    )
    depth = history_shard_ref.shape[0]
    half = groups // 2
    row, core = lax.div(group, half), lax.rem(group, 2)
    across = lax.rem(group + half, groups)
    beside = [row * half + lax.rem(group - row * half + 2 * d, half) for d in range(1, half // 2)]
    diagonal = [lax.rem(source + half, groups) for source in beside]
    near = (*beside, across)
    same_core = (*near, *diagonal)
    partner_core = [source + partner - group for source in same_core]
    others = [lax.rem(shard + d, shards) for d in range(1, shards)]
    last = shards - 1
    relays = ((1, last, 0), (last - 1, 0, last)) if shards > 2 else ()
    lead = requests // 2
    ahead = lead // 2

    def rows_of(source):
        return pl.ds(pl.multiple_of(source * depth, depth), depth)

    def events_of(source):
        return pl.ds(pl.multiple_of(source * own_events, own_events), own_events)

    def weight_copy(w, target, source, send):
        part, full = weights[w]
        return pltpu.make_async_remote_copy(
            src_ref=part,
            dst_ref=full.at[rows_of(source)],
            send_sem=send,
            recv_sem=weight_recv.at[w, source],
            device_id={"req": target},
            device_id_type=MESH,
        )

    def pass_copy(w, k, source):
        full = weights[w][1]
        return pltpu.make_async_remote_copy(
            src_ref=full.at[rows_of(source)],
            dst_ref=full.at[rows_of(source)],
            send_sem=pass_send.at[w, k],
            recv_sem=weight_recv.at[w, source],
            device_id={"req": partner},
            device_id_type=MESH,
        )

    def turn_copy(w, k):
        full = weights[w][1]
        source = beside[k] + core * (across - beside[k])
        target = across + core * (beside[k] - across)
        return pltpu.make_async_remote_copy(
            src_ref=full.at[rows_of(source)],
            dst_ref=full.at[rows_of(source)],
            send_sem=turn_send.at[w, k],
            recv_sem=weight_recv.at[w, source],
            device_id={"req": target},
            device_id_type=MESH,
        )

    def relay_copy(i, k):
        _, source, target = relays[k]
        return pltpu.make_async_remote_copy(
            src_ref=events_ref.at[i, events_of(source)],
            dst_ref=events_ref.at[i, events_of(source)],
            send_sem=event_send.at[i, len(others) + k],
            recv_sem=event_recv.at[i, source],
            device_id={"cand": target},
            device_id_type=MESH,
        )

    def is_far(target):
        return (shards > 2) & (jnp.abs(target - shard) == last)

    def is_relayed(source):
        flag = shard < 0
        for middle, start, _ in relays:
            flag = flag | ((shard == middle) & (source == start))
        return flag

    def relay(i):
        for k, (middle, source, _) in enumerate(relays):

            @pl.when(shard == middle)
            def _():
                event_copy(i, 0, 0, source).wait_recv()
                relay_copy(i, k).start()

    def event_copy(i, k, target, source):
        return pltpu.make_async_remote_copy(
            src_ref=history_ref.at[i],
            dst_ref=events_ref.at[i, events_of(source)],
            send_sem=event_send.at[i, k],
            recv_sem=event_recv.at[i, source],
            device_id={"cand": target},
            device_id_type=MESH,
        )

    def logit_copy(i, k, target, source):
        return pltpu.make_async_remote_copy(
            src_ref=logits_ref.at[source, i],
            dst_ref=logits_ref.at[source, i],
            send_sem=logit_send.at[i, k],
            recv_sem=logit_recv.at[i, source],
            device_id={"cand": target},
            device_id_type=MESH,
        )

    def own_weight(w):
        part, full = weights[w]
        return pltpu.make_async_copy(part, full.at[rows_of(group)], own_sem.at[w])

    def own_event(i):
        return pltpu.make_async_copy(
            history_ref.at[i], events_ref.at[i, events_of(shard)], own_sem.at[len(weights) + i]
        )

    barrier = pltpu.get_barrier_semaphore()
    for target in (*near, partner):
        pl.semaphore_signal(barrier, inc=1, device_id={"req": target}, device_id_type=MESH)
    for target in others:
        pl.semaphore_signal(barrier, inc=1, device_id={"cand": target}, device_id_type=MESH)
    pl.semaphore_wait(barrier, len(near) + 1 + len(others))

    def send(w):
        for k, target in enumerate((*near, partner)):
            weight_copy(w, target, group, weight_send.at[w, k]).start()
        own_weight(w).start()

    send(0)
    send(1)

    @pl.loop(0, requests)
    def _(i):
        for k, target in enumerate(others):

            @pl.when(jnp.logical_not(is_far(target)))
            def _():
                event_copy(i, k, target, shard).start()

        own_event(i).start()

    def pass_on(w, sources, first):
        for k, source in enumerate(sources):
            pass_copy(w, first + k, source).start()

    def arrive(w, sources):
        for source in sources:
            weight_copy(w, partner, source, weight_send.at[w, 0]).wait_recv()

    def turn(w):
        arrive(w, near)
        for k in range(len(beside)):
            turn_copy(w, k).start()
        pass_on(w, near, 0)

    def settle(w):
        arrive(w, diagonal)
        pass_on(w, diagonal, len(near))
        own_weight(w).wait()
        arrive(w, (partner, *partner_core))

    turn(0)
    for w in range(2, len(weights)):
        send(w)
    turn(1)
    settle(0)
    query_ref[...] = silu(
        jnp.dot(
            items_ref[...], candidate_weight_ref[:, :width], preferred_element_type=jnp.float32
        )
    ).astype(jnp.bfloat16)
    gate_ref[...] = (
        silu(
            jnp.dot(
                items_ref[...], candidate_weight_ref[:, width:], preferred_element_type=jnp.float32
            )
        )
        * gain_ref[...]
    )
    relay(0)
    settle(1)
    for w in range(2, len(weights)):
        turn(w)
    for i in range(1, ahead):
        relay(i)
    for w in range(2, len(weights)):
        settle(w)
    for i in range(max(1, ahead), lead):
        relay(i)

    @pl.loop(0, requests)
    def _(i):
        @pl.when((i >= lead - ahead) & (i + ahead < requests))
        def _():
            relay(i + ahead)

        own_event(i).wait()
        for k, source in enumerate(others):

            @pl.when(jnp.logical_not(is_relayed(source)))
            def _():
                event_copy(i, k, source, source).wait_recv()

        length = length_ref[i]
        inverse = 1.0 / jnp.full((1, 1), length, jnp.int32).astype(jnp.float32)
        pairs_ref[:, :width] = silu(
            jnp.dot(
                events_ref[i], history_weight_ref[:, :width], preferred_element_type=jnp.float32
            )
        ).astype(jnp.bfloat16)
        live = lax.broadcasted_iota(jnp.int32, (history_total, width), 0) < length
        pairs_ref[:, width:] = jnp.where(
            live,
            silu(
                jnp.dot(
                    events_ref[i], history_weight_ref[:, width:], preferred_element_type=jnp.float32
                )
            ),
            0.0,
        ).astype(jnp.bfloat16)
        for h in range(HEADS):
            part = slice(h * head, (h + 1) * head)
            scores = half_scale * lax.dot_general(
                query_ref[:, part],
                pairs_ref[:, part],
                (((1,), (1,)), ((), ())),
                preferred_element_type=jnp.float32,
            )
            mixed = ((scores + scores * jnp.tanh(scores)) * inverse).astype(jnp.bfloat16)
            attended_ref[:, part] = jnp.dot(
                mixed,
                pairs_ref[:, width + h * head : width + (h + 1) * head],
                preferred_element_type=jnp.float32,
            )

        @pl.when(i > 0)
        def _():
            for k, target in enumerate(others):
                logit_copy(i - 1, k, target, shard).start()

        attended = attended_ref[...]
        center = attended - jnp.mean(attended, axis=-1, keepdims=True)
        spread = jnp.mean(center * center, axis=-1, keepdims=True)
        normed = (center * lax.rsqrt(spread + EPSILON) * gate_ref[...]).astype(jnp.bfloat16)
        merged = (
            jnp.dot(normed, output_weight_ref[...], preferred_element_type=jnp.float32)
            + items_ref[...].astype(jnp.float32)
        ).astype(jnp.bfloat16)
        hidden = silu(
            jnp.dot(merged, hidden_weight_ref[...], preferred_element_type=jnp.float32)
        ).astype(jnp.bfloat16)
        logits_ref[shard, i] = lax.dot_general(
            score_weight_ref[...],
            hidden,
            (((1,), (1,)), ((), ())),
            preferred_element_type=jnp.float32,
        )

    for w in range(len(weights)):
        for k, target in enumerate((*near, partner)):
            weight_copy(w, target, group, weight_send.at[w, k]).wait_send()
        for k, source in enumerate(same_core):
            pass_copy(w, k, source).wait_send()
        for k in range(len(beside)):
            turn_copy(w, k).wait_send()

    @pl.loop(0, requests)
    def _(i):
        for k, target in enumerate(others):

            @pl.when(jnp.logical_not(is_far(target)))
            def _():
                event_copy(i, k, target, shard).wait_send()

        for k, (middle, _, _) in enumerate(relays):

            @pl.when(shard == middle)
            def _():
                relay_copy(i, k).wait_send()

    for k, target in enumerate(others):
        logit_copy(requests - 1, k, target, shard).start()

    @pl.loop(0, requests)
    def _(i):
        for k, target in enumerate(others):
            logit_copy(i, k, target, shard).wait_send()
            logit_copy(i, k, target, target).wait_recv()


def pair_logits(
    history, length, items, history_weight, candidate_weight, output_weight, hidden_weight, gain,
    score_weight,
):
    requests, own_events, width = history.shape
    rows = items.shape[0]
    groups, shards = lax.axis_size("req"), lax.axis_size("cand")
    history_total = own_events * shards
    whole = pl.BlockSpec(memory_space=pltpu.VMEM)
    apart = pl.BlockSpec(memory_space=pl.ANY)
    weights = (history_weight, candidate_weight, output_weight, hidden_weight)
    count = len(weights)
    return pl.pallas_call(
        functools.partial(pair_kernel, groups, shards),
        out_shape=jax.ShapeDtypeStruct((shards, requests, score_weight.shape[0], rows), jnp.float32),
        in_specs=[
            pl.BlockSpec(memory_space=pltpu.SMEM),
            apart, whole, apart, apart, apart, apart, whole, whole,
        ],
        out_specs=whole,
        scratch_shapes=[
            pltpu.VMEM((requests, history_total, width), jnp.bfloat16),
            *(
                pltpu.VMEM((weight.shape[0] * groups, weight.shape[1]), jnp.bfloat16)
                for weight in weights
            ),
            pltpu.VMEM((rows, width), jnp.bfloat16),
            pltpu.VMEM((rows, width), jnp.float32),
            pltpu.VMEM((history_total, 2 * width), jnp.bfloat16),
            pltpu.VMEM((rows, width), jnp.float32),
            pltpu.SemaphoreType.DMA((count, groups // 2)),
            pltpu.SemaphoreType.DMA((count, groups)),
            pltpu.SemaphoreType.DMA((count, groups // 2)),
            pltpu.SemaphoreType.DMA((count, groups // 2)),
            pltpu.SemaphoreType.DMA((requests, shards + 1)),
            pltpu.SemaphoreType.DMA((requests, shards)),
            pltpu.SemaphoreType.DMA((requests, shards)),
            pltpu.SemaphoreType.DMA((requests, shards)),
            pltpu.SemaphoreType.DMA((count + requests,)),
        ],
        compiler_params=pltpu.CompilerParams(
            collective_id=0, has_side_effects=True, vmem_limit_bytes=58 * 1024 * 1024
        ),
    )(
        length, history, items, history_weight, candidate_weight, output_weight, hidden_weight,
        gain, score_weight,
    )


def blend(logits, candidate_count, block_shard, block_index, item_ages, item_blocks):
    shards = lax.axis_size("cand")
    mine = lax.axis_index("cand")
    requests, max_blocks = block_shard.shape
    per_scorer = max_blocks // shards
    logits = logits.reshape(shards, requests, -1, item_blocks, BLOCK)
    ids = lax.dynamic_slice_in_dim(
        block_shard * item_blocks + block_index, mine * per_scorer, per_scorer, 1
    )
    names = jnp.arange(shards * item_blocks, dtype=jnp.int32).reshape(shards, 1, 1, item_blocks, 1)
    picked = ids[None, :, :, None, None] == names
    first, second = (
        jnp.sum(jnp.where(picked, logits[:, :, None, c], 0.0), axis=(0, 3)) for c in (0, 1)
    )
    decays = jnp.exp(
        -item_ages.astype(jnp.float32).reshape(requests, per_scorer, BLOCK) / AGE_SCALE
    )
    blended = decays * first + (1.0 - decays) * second
    row_number = (mine * per_scorer + jnp.arange(per_scorer, dtype=jnp.int32))[
        None, :, None
    ] * BLOCK + jnp.arange(BLOCK, dtype=jnp.int32)[None, None, :]
    kept_rows = row_number < candidate_count[:, None, None]
    return jnp.where(kept_rows, blended, 0.0).reshape(requests, per_scorer * BLOCK)


def local(
    history,
    history_length,
    candidate_count,
    block_shard,
    block_index,
    item_table,
    item_ages,
    history_weight,
    candidate_weight,
    output_weight,
    hidden_weight,
    norm_gain,
    score_weight,
):
    item_blocks = item_table.shape[0]
    logits = pair_logits(
        history,
        history_length,
        item_table.reshape(-1, item_table.shape[2]),
        history_weight,
        candidate_weight,
        output_weight,
        hidden_weight,
        norm_gain[None, :],
        score_weight,
    )
    return blend(logits, candidate_count, block_shard, block_index, item_ages, item_blocks)


def solution(mesh):
    return jax.shard_map(
        local,
        mesh=mesh,
        in_specs=(
            P("req", "cand", None),
            P("req"),
            P("req"),
            P("req", None),
            P("req", None),
            P("cand", None, None),
            P("req", "cand"),
            P("req", None),
            P("req", None),
            P("req", None),
            P("req", None),
            P(),
            P(),
        ),
        out_specs=P("req", "cand"),
        check_vma=False,
    )
```

```python
import functools
import math

import jax
import jax.numpy as jnp
from jax import lax
from jax.experimental import pallas as pl
from jax.experimental.pallas import tpu as pltpu
from jax.sharding import PartitionSpec as P

HEADS = 8
BLOCK = 128
EPSILON = 1e-05
AGE_SCALE = 48.0


def silu(value):
    half = 0.5 * value
    return half + half * jnp.tanh(half)


MESH = pl.DeviceIdType.MESH


def pair_kernel(
    groups,
    shards,
    length_ref,
    history_ref,
    items_ref,
    history_shard_ref,
    candidate_shard_ref,
    output_shard_ref,
    hidden_shard_ref,
    gain_ref,
    score_weight_ref,
    logits_ref,
    events_ref,
    history_weight_ref,
    candidate_weight_ref,
    output_weight_ref,
    hidden_weight_ref,
    query_ref,
    gate_ref,
    pairs_ref,
    attended_ref,
    weight_send,
    weight_recv,
    pass_send,
    turn_send,
    event_send,
    event_recv,
    logit_send,
    logit_recv,
    own_sem,
):
    group = lax.axis_index("req")
    shard = lax.axis_index("cand")
    partner = group + 1 - 2 * lax.rem(group, 2)
    requests, own_events, width = history_ref.shape
    history_total = events_ref.shape[1]
    head = width // HEADS
    half_scale = 0.5 / math.sqrt(head)
    weights = (
        (candidate_shard_ref, candidate_weight_ref),
        (history_shard_ref, history_weight_ref),
        (output_shard_ref, output_weight_ref),
        (hidden_shard_ref, hidden_weight_ref),
    )
    depth = history_shard_ref.shape[0]
    half = groups // 2
    row, core = lax.div(group, half), lax.rem(group, 2)
    across = lax.rem(group + half, groups)
    beside = [row * half + lax.rem(group - row * half + 2 * d, half) for d in range(1, half // 2)]
    diagonal = [lax.rem(source + half, groups) for source in beside]
    near = (*beside, across)
    same_core = (*near, *diagonal)
    partner_core = [source + partner - group for source in same_core]
    others = [lax.rem(shard + d, shards) for d in range(1, shards)]
    last = shards - 1
    relays = ((1, last, 0), (last - 1, 0, last)) if shards > 2 else ()
    lead = requests // 2
    ahead = lead // 2

    def rows_of(source):
        return pl.ds(pl.multiple_of(source * depth, depth), depth)

    def events_of(source):
        return pl.ds(pl.multiple_of(source * own_events, own_events), own_events)

    def weight_copy(w, target, source, send):
        part, full = weights[w]
        return pltpu.make_async_remote_copy(
            src_ref=part,
            dst_ref=full.at[rows_of(source)],
            send_sem=send,
            recv_sem=weight_recv.at[w, source],
            device_id={"req": target},
            device_id_type=MESH,
        )

    def pass_copy(w, k, source):
        full = weights[w][1]
        return pltpu.make_async_remote_copy(
            src_ref=full.at[rows_of(source)],
            dst_ref=full.at[rows_of(source)],
            send_sem=pass_send.at[w, k],
            recv_sem=weight_recv.at[w, source],
            device_id={"req": partner},
            device_id_type=MESH,
        )

    def turn_copy(w, k):
        full = weights[w][1]
        source = beside[k] + core * (across - beside[k])
        target = across + core * (beside[k] - across)
        return pltpu.make_async_remote_copy(
            src_ref=full.at[rows_of(source)],
            dst_ref=full.at[rows_of(source)],
            send_sem=turn_send.at[w, k],
            recv_sem=weight_recv.at[w, source],
            device_id={"req": target},
            device_id_type=MESH,
        )

    def relay_copy(i, k):
        _, source, target = relays[k]
        return pltpu.make_async_remote_copy(
            src_ref=events_ref.at[i, events_of(source)],
            dst_ref=events_ref.at[i, events_of(source)],
            send_sem=event_send.at[i, len(others) + k],
            recv_sem=event_recv.at[i, source],
            device_id={"cand": target},
            device_id_type=MESH,
        )

    def is_far(target):
        return (shards > 2) & (jnp.abs(target - shard) == last)

    def is_relayed(source):
        flag = shard < 0
        for middle, start, _ in relays:
            flag = flag | ((shard == middle) & (source == start))
        return flag

    def relay(i):
        for k, (middle, source, _) in enumerate(relays):

            @pl.when(shard == middle)
            def _():
                event_copy(i, 0, 0, source).wait_recv()
                relay_copy(i, k).start()

    def event_copy(i, k, target, source):
        return pltpu.make_async_remote_copy(
            src_ref=history_ref.at[i],
            dst_ref=events_ref.at[i, events_of(source)],
            send_sem=event_send.at[i, k],
            recv_sem=event_recv.at[i, source],
            device_id={"cand": target},
            device_id_type=MESH,
        )

    def logit_copy(i, k, target, source):
        return pltpu.make_async_remote_copy(
            src_ref=logits_ref.at[source, i],
            dst_ref=logits_ref.at[source, i],
            send_sem=logit_send.at[i, k],
            recv_sem=logit_recv.at[i, source],
            device_id={"cand": target},
            device_id_type=MESH,
        )

    def own_weight(w):
        part, full = weights[w]
        return pltpu.make_async_copy(part, full.at[rows_of(group)], own_sem.at[w])

    def own_event(i):
        return pltpu.make_async_copy(
            history_ref.at[i], events_ref.at[i, events_of(shard)], own_sem.at[len(weights) + i]
        )

    barrier = pltpu.get_barrier_semaphore()
    for target in (*near, partner):
        pl.semaphore_signal(barrier, inc=1, device_id={"req": target}, device_id_type=MESH)
    for target in others:
        pl.semaphore_signal(barrier, inc=1, device_id={"cand": target}, device_id_type=MESH)
    pl.semaphore_wait(barrier, len(near) + 1 + len(others))

    def send(w):
        for k, target in enumerate((*near, partner)):
            weight_copy(w, target, group, weight_send.at[w, k]).start()
        own_weight(w).start()

    send(0)
    send(1)

    @pl.loop(0, requests)
    def _(i):
        for k, target in enumerate(others):

            @pl.when(jnp.logical_not(is_far(target)))
            def _():
                event_copy(i, k, target, shard).start()

        own_event(i).start()

    def pass_on(w, sources, first):
        for k, source in enumerate(sources):
            pass_copy(w, first + k, source).start()

    def arrive(w, sources):
        for source in sources:
            weight_copy(w, partner, source, weight_send.at[w, 0]).wait_recv()

    def turn(w):
        arrive(w, near)
        for k in range(len(beside)):
            turn_copy(w, k).start()
        pass_on(w, near, 0)

    def settle(w):
        arrive(w, diagonal)
        pass_on(w, diagonal, len(near))
        own_weight(w).wait()
        arrive(w, (partner, *partner_core))

    turn(0)
    for w in range(2, len(weights)):
        send(w)
    turn(1)
    settle(0)
    query_ref[...] = silu(
        jnp.dot(
            items_ref[...], candidate_weight_ref[:, :width], preferred_element_type=jnp.float32
        )
    ).astype(jnp.bfloat16)
    gate_ref[...] = (
        silu(
            jnp.dot(
                items_ref[...], candidate_weight_ref[:, width:], preferred_element_type=jnp.float32
            )
        )
        * gain_ref[...]
    )
    def project(i):
        own_event(i).wait()
        for k, source in enumerate(others):

            @pl.when(jnp.logical_not(is_relayed(source)))
            def _():
                event_copy(i, k, source, source).wait_recv()

        pairs_ref[i, :, :width] = silu(
            jnp.dot(
                events_ref[i], history_weight_ref[:, :width], preferred_element_type=jnp.float32
            )
        ).astype(jnp.bfloat16)
        live = lax.broadcasted_iota(jnp.int32, (history_total, width), 0) < length_ref[i]
        pairs_ref[i, :, width:] = jnp.where(
            live,
            silu(
                jnp.dot(
                    events_ref[i], history_weight_ref[:, width:], preferred_element_type=jnp.float32
                )
            ),
            0.0,
        ).astype(jnp.bfloat16)
    relay(0)
    settle(1)
    for i in range(1, ahead):
        relay(i)
    ready = 0
    for w in range(2, len(weights)):
        turn(w)
        for i in range(ready, ready + lead // 4):
            project(i)
        ready += lead // 4
    for i in range(ahead, lead):
        relay(i)
    for i in range(ready, lead):
        project(i)
    for w in range(2, len(weights)):
        settle(w)

    @pl.loop(0, requests)
    def _(i):
        @pl.when((i >= lead - ahead) & (i + ahead < requests))
        def _():
            relay(i + ahead)

        @pl.when(i >= lead)
        def _():
            project(i)

        length = length_ref[i]
        inverse = 1.0 / jnp.full((1, 1), length, jnp.int32).astype(jnp.float32)
        for h in range(HEADS):
            part = slice(h * head, (h + 1) * head)
            scores = half_scale * lax.dot_general(
                query_ref[:, part],
                pairs_ref[i, :, part],
                (((1,), (1,)), ((), ())),
                preferred_element_type=jnp.float32,
            )
            mixed = ((scores + scores * jnp.tanh(scores)) * inverse).astype(jnp.bfloat16)
            attended_ref[:, part] = jnp.dot(
                mixed,
                pairs_ref[i, :, width + h * head : width + (h + 1) * head],
                preferred_element_type=jnp.float32,
            )

        @pl.when(i > 0)
        def _():
            for k, target in enumerate(others):
                logit_copy(i - 1, k, target, shard).start()

        attended = attended_ref[...]
        center = attended - jnp.mean(attended, axis=-1, keepdims=True)
        spread = jnp.mean(center * center, axis=-1, keepdims=True)
        normed = (center * lax.rsqrt(spread + EPSILON) * gate_ref[...]).astype(jnp.bfloat16)
        merged = (
            jnp.dot(normed, output_weight_ref[...], preferred_element_type=jnp.float32)
            + items_ref[...].astype(jnp.float32)
        ).astype(jnp.bfloat16)
        hidden = silu(
            jnp.dot(merged, hidden_weight_ref[...], preferred_element_type=jnp.float32)
        ).astype(jnp.bfloat16)
        logits_ref[shard, i] = lax.dot_general(
            score_weight_ref[...],
            hidden,
            (((1,), (1,)), ((), ())),
            preferred_element_type=jnp.float32,
        )

    for w in range(len(weights)):
        for k, target in enumerate((*near, partner)):
            weight_copy(w, target, group, weight_send.at[w, k]).wait_send()
        for k, source in enumerate(same_core):
            pass_copy(w, k, source).wait_send()
        for k in range(len(beside)):
            turn_copy(w, k).wait_send()

    @pl.loop(0, requests)
    def _(i):
        for k, target in enumerate(others):

            @pl.when(jnp.logical_not(is_far(target)))
            def _():
                event_copy(i, k, target, shard).wait_send()

        for k, (middle, _, _) in enumerate(relays):

            @pl.when(shard == middle)
            def _():
                relay_copy(i, k).wait_send()

    for k, target in enumerate(others):
        logit_copy(requests - 1, k, target, shard).start()

    @pl.loop(0, requests)
    def _(i):
        for k, target in enumerate(others):
            logit_copy(i, k, target, shard).wait_send()
            logit_copy(i, k, target, target).wait_recv()


def pair_logits(
    history, length, items, history_weight, candidate_weight, output_weight, hidden_weight, gain,
    score_weight,
):
    requests, own_events, width = history.shape
    rows = items.shape[0]
    groups, shards = lax.axis_size("req"), lax.axis_size("cand")
    history_total = own_events * shards
    whole = pl.BlockSpec(memory_space=pltpu.VMEM)
    apart = pl.BlockSpec(memory_space=pl.ANY)
    weights = (history_weight, candidate_weight, output_weight, hidden_weight)
    count = len(weights)
    return pl.pallas_call(
        functools.partial(pair_kernel, groups, shards),
        out_shape=jax.ShapeDtypeStruct((shards, requests, score_weight.shape[0], rows), jnp.float32),
        in_specs=[
            pl.BlockSpec(memory_space=pltpu.SMEM),
            apart, whole, apart, apart, apart, apart, whole, whole,
        ],
        out_specs=whole,
        scratch_shapes=[
            pltpu.VMEM((requests, history_total, width), jnp.bfloat16),
            *(
                pltpu.VMEM((weight.shape[0] * groups, weight.shape[1]), jnp.bfloat16)
                for weight in weights
            ),
            pltpu.VMEM((rows, width), jnp.bfloat16),
            pltpu.VMEM((rows, width), jnp.float32),
            pltpu.VMEM((requests, history_total, 2 * width), jnp.bfloat16),
            pltpu.VMEM((rows, width), jnp.float32),
            pltpu.SemaphoreType.DMA((count, groups // 2)),
            pltpu.SemaphoreType.DMA((count, groups)),
            pltpu.SemaphoreType.DMA((count, groups // 2)),
            pltpu.SemaphoreType.DMA((count, groups // 2)),
            pltpu.SemaphoreType.DMA((requests, shards + 1)),
            pltpu.SemaphoreType.DMA((requests, shards)),
            pltpu.SemaphoreType.DMA((requests, shards)),
            pltpu.SemaphoreType.DMA((requests, shards)),
            pltpu.SemaphoreType.DMA((count + requests,)),
        ],
        compiler_params=pltpu.CompilerParams(
            collective_id=0, has_side_effects=True, vmem_limit_bytes=58 * 1024 * 1024
        ),
    )(
        length, history, items, history_weight, candidate_weight, output_weight, hidden_weight,
        gain, score_weight,
    )


def blend(logits, candidate_count, block_shard, block_index, item_ages, item_blocks):
    shards = lax.axis_size("cand")
    mine = lax.axis_index("cand")
    requests, max_blocks = block_shard.shape
    per_scorer = max_blocks // shards
    logits = logits.reshape(shards, requests, -1, item_blocks, BLOCK)
    ids = lax.dynamic_slice_in_dim(
        block_shard * item_blocks + block_index, mine * per_scorer, per_scorer, 1
    )
    names = jnp.arange(shards * item_blocks, dtype=jnp.int32).reshape(shards, 1, 1, item_blocks, 1)
    picked = ids[None, :, :, None, None] == names
    first, second = (
        jnp.sum(jnp.where(picked, logits[:, :, None, c], 0.0), axis=(0, 3)) for c in (0, 1)
    )
    decays = jnp.exp(
        -item_ages.astype(jnp.float32).reshape(requests, per_scorer, BLOCK) / AGE_SCALE
    )
    blended = decays * first + (1.0 - decays) * second
    row_number = (mine * per_scorer + jnp.arange(per_scorer, dtype=jnp.int32))[
        None, :, None
    ] * BLOCK + jnp.arange(BLOCK, dtype=jnp.int32)[None, None, :]
    kept_rows = row_number < candidate_count[:, None, None]
    return jnp.where(kept_rows, blended, 0.0).reshape(requests, per_scorer * BLOCK)


def local(
    history,
    history_length,
    candidate_count,
    block_shard,
    block_index,
    item_table,
    item_ages,
    history_weight,
    candidate_weight,
    output_weight,
    hidden_weight,
    norm_gain,
    score_weight,
):
    item_blocks = item_table.shape[0]
    logits = pair_logits(
        history,
        history_length,
        item_table.reshape(-1, item_table.shape[2]),
        history_weight,
        candidate_weight,
        output_weight,
        hidden_weight,
        norm_gain[None, :],
        score_weight,
    )
    return blend(logits, candidate_count, block_shard, block_index, item_ages, item_blocks)


def solution(mesh):
    return jax.shard_map(
        local,
        mesh=mesh,
        in_specs=(
            P("req", "cand", None),
            P("req"),
            P("req"),
            P("req", None),
            P("req", None),
            P("cand", None, None),
            P("req", "cand"),
            P("req", None),
            P("req", None),
            P("req", None),
            P("req", None),
            P(),
            P(),
        ),
        out_specs=P("req", "cand"),
        check_vma=False,
    )
```
